32 devices in a mesh: fsdp: 8 (over z, core), tp: 4 (over y, x).
Axes of the slice: x: 2, y: 2, z: 4, core: 2. Of those that a mesh axis runs over, the one named last changes fastest.
Arguments:
- hidden: bfloat16 [8192, 14336], P('fsdp', 'tp'), may hold values from -6 to 6
- grad_out: bfloat16 [8192, 4096], P('fsdp'), may hold values from -0.09375 to 0.09375
- master: float32 [4096, 14336], P('fsdp', 'tp'), may hold values from -0.046875 to 0.046875
- moment_one: float32 [4096, 14336], P('fsdp', 'tp'), may hold values from -3 to 3
- moment_two: float32 [4096, 14336], P('fsdp', 'tp'), may hold values from 0.1 to 4
Outputs:
- new_master: float32 [4096, 14336], P('fsdp', 'tp')
- new_one: float32 [4096, 14336], P('fsdp', 'tp')
- new_two: float32 [4096, 14336], P('fsdp', 'tp')
- quantized: bfloat16 [4096, 14336], P(None, 'fsdp')
- block_scales: bfloat16 [32, 112], P(None, 'fsdp')
The draws below stay inside these ranges and needn't reach their ends.
All inputs are finite; a program needn't handle non-finite values.
Results may differ from the reference program's by a relative error of at most 0.0051.
Values may be sent and summed in bfloat16 or wider, within the bound.
No kernel may reach another device: no remote copies, remote signals or barrier semaphores. Data moves between devices by JAX's collectives and lax.ppermute only.
A program may use at most 192 MiB of HBM per device.

```python
import math
import jax
import jax.numpy as jnp
from jax import lax

DMOD = 4096
FFN = 14336
BLOCK = 128
TOKENS = 8192


def strengthened(array, own_key, source, target, shards_of, factor):
    def block_of(dim):
        return (jnp.arange(array.shape[dim]) // (array.shape[dim] // shards_of)).reshape((-1,) + (1,) * (array.ndim - 1 - dim))

    first = jax.random.permutation(own_key, shards_of)[block_of(target)]
    other_side = (block_of(target) + shards_of // 2) % shards_of
    return jnp.where((block_of(source) == first) | (block_of(source) == other_side), factor * array, array)


def levels(stream_key, shape, split, least, largest):
    gain = 1.0
    for position, parts in split:
        steps = jax.random.uniform(jax.random.fold_in(jax.random.fold_in(stream_key, 6), position), (parts,), jnp.float32, least / len(split), largest / len(split))
        gain = gain * jnp.repeat(jnp.exp(steps), shape[position] // parts).reshape((-1,) + (1,) * (len(shape) - 1 - position))
    return gain


def normal_values(stream_key, extent, spread, bound, pieces=(), kind=jnp.bfloat16):
    level = levels(stream_key, extent, pieces, -0.22, 0.18) if pieces else 1.0
    result = jax.random.normal(stream_key, extent, jnp.float32) * spread * level
    return jnp.minimum(jnp.maximum(result, -bound), bound).astype(kind)


def noise_with(rng, extent, width, limit, shards, heavy, held_as=jnp.bfloat16):
    array = width * jax.random.normal(rng, extent, jnp.float32)
    if shards:
        array = array * levels(rng, extent, shards, -0.22, 0.18)
    return jnp.clip(strengthened(array, jax.random.fold_in(rng, 3), *heavy), -limit, limit).astype(held_as)


def setup_inputs(seed: int = 0) -> dict:
    key_list = jax.random.split(jax.random.key(seed), 6)
    hidden = normal_values(key_list[0], (TOKENS, FFN), 1.0, 6.0, ((0, 8), (1, 4)))
    grad_out = noise_with(key_list[1], (TOKENS, DMOD), TOKENS ** -0.5, 0.09375, ((0, 8),), (0, 1, 8, 2.0))
    master = normal_values(key_list[2], (DMOD, FFN), FFN ** -0.5, 0.046875, ((0, 8), (1, 4)), jnp.float32)
    moment_one = normal_values(key_list[3], (DMOD, FFN), 0.5, 3.0, ((0, 8), (1, 4)), jnp.float32)
    moment_two = jnp.clip(jnp.exp(math.log(4.0) - 3.6888794 * jax.random.uniform(key_list[4], (DMOD, FFN), jnp.float32) ** levels(key_list[4], (DMOD, FFN), ((0, 8), (1, 4)), -0.2, 0.2)), 0.1, 4.0)
    return {"hidden": hidden, "grad_out": grad_out, "master": master, "moment_one": moment_one, "moment_two": moment_two}


beta_one = 0.9
beta_two = 0.95
learn_rate = 0.005
adam_eps = 1e-08
scale_eps = 1e-06
steps_done = 4

def quantize(weights):
    rows, cols = weights.shape
    blocks = weights.reshape(rows // BLOCK, BLOCK, cols // BLOCK, BLOCK)
    peak = lax.optimization_barrier(jnp.max(jnp.abs(blocks), axis=(1, 3))) + scale_eps
    scales = peak.astype(jnp.bfloat16)
    widened = lax.optimization_barrier(scales).astype(jnp.float32)
    values = (blocks / widened[:, None, :, None]).reshape(rows, cols).astype(jnp.bfloat16)
    return (values, scales)

def reference(hidden, grad_out, master, moment_one, moment_two):
    grad = jnp.dot(grad_out.T, hidden, preferred_element_type=jnp.float32)
    new_one = beta_one * moment_one + (1.0 - beta_one) * grad
    new_two = beta_two * moment_two + (1.0 - beta_two) * grad * grad
    fix_one = 1.0 - beta_one ** steps_done
    fix_two = 1.0 - beta_two ** steps_done
    new_master = master - learn_rate * (new_one / fix_one) / (jnp.sqrt(new_two / fix_two) + adam_eps)
    quantized, block_scales = quantize(new_master)
    return (new_master, new_one, new_two, quantized, block_scales)
```

```python
import functools
import itertools

import jax
import jax.numpy as jnp
from jax import lax
from jax.experimental import pallas as pl
from jax.experimental.pallas import tpu as pltpu
from jax.sharding import PartitionSpec as P


BLOCK = 128
SCALE_ROWS = 16

beta_one = 0.9
beta_two = 0.95
learn_rate = 0.005
adam_eps = 1e-08
scale_eps = 1e-06
steps_done = 4
fix_one = 1.0 - beta_one**steps_done
fix_two = 1.0 - beta_two**steps_done

AXES = ("fsdp", "tp")


def turn_kernel(table, source, target):
    target[0] = source[...].T


def turned(table, grad_out, rows):
    tokens, places = grad_out.shape[0], table.shape[0]
    return pl.pallas_call(
        turn_kernel,
        grid_spec=pltpu.PrefetchScalarGridSpec(
            num_scalar_prefetch=1,
            grid=(places,),
            in_specs=[pl.BlockSpec((tokens, rows), lambda s, tab: (0, tab[s]))],
            out_specs=pl.BlockSpec((1, rows, tokens), lambda s, tab: (s, 0, 0)),
        ),
        out_shape=jax.ShapeDtypeStruct((places, rows, tokens), grad_out.dtype),
        cost_estimate=pl.CostEstimate(flops=0, bytes_accessed=4 * tokens * places * rows, transcendentals=0),
        name="turn",
    )(table, grad_out)


def product_kernel(table, own_go, peer_go, own_lo, own_hi, peer_lo, peer_hi, sends, own, right):
    slot, last = pl.program_id(0), pl.num_programs(0) - 1
    width = own_lo.shape[1]

    @pl.when(slot == 0)
    def _():
        for which, (lo, hi) in enumerate(((own_lo, own_hi), (peer_lo, peer_hi))):
            right[which, :, :width] = lo[...]
            right[which, :, width:] = hi[...]

    total = jnp.dot(own_go[0], right[0], preferred_element_type=jnp.float32)
    total += jnp.dot(peer_go[0], right[1], preferred_element_type=jnp.float32)

    @pl.when(slot < last)
    def _():
        sends[0] = total.astype(sends.dtype)

    @pl.when(slot == last)
    def _():
        own[...] = total


def partial_products(at, table, grad_out, peer_grad, hidden, peer_hidden):
    j, chunks, width = at
    tokens, (places, rows) = hidden.shape[0], grad_out.shape[:2]
    lo, hi = lambda s, tab: (0, j), lambda s, tab: (0, chunks + j)
    turned_spec = pl.BlockSpec((1, rows, tokens), lambda s, tab: (tab[s], 0, 0))
    return pl.pallas_call(
        product_kernel,
        grid_spec=pltpu.PrefetchScalarGridSpec(
            num_scalar_prefetch=1,
            grid=(places,),
            in_specs=[
                turned_spec,
                turned_spec,
                pl.BlockSpec((tokens, width), lo),
                pl.BlockSpec((tokens, width), hi),
                pl.BlockSpec((tokens, width), lo),
                pl.BlockSpec((tokens, width), hi),
            ],
            out_specs=[
                pl.BlockSpec((1, rows, 2 * width), lambda s, tab: (jnp.minimum(s, places - 2), 0, 0)),
                pl.BlockSpec((rows, 2 * width), lambda s, tab: (0, 0)),
            ],
            scratch_shapes=[pltpu.VMEM((2, tokens, 2 * width), jnp.bfloat16)],
        ),
        out_shape=[
            jax.ShapeDtypeStruct((places - 1, rows, 2 * width), jnp.bfloat16),
            jax.ShapeDtypeStruct((rows, 2 * width), jnp.float32),
        ],
        cost_estimate=pl.CostEstimate(
            flops=8 * tokens * places * rows * width,
            bytes_accessed=4 * tokens * places * rows + 8 * tokens * width + 4 * places * rows * width,
            transcendentals=0,
        ),
        name="products",
    )(table, grad_out, peer_grad, hidden, hidden, peer_hidden, peer_hidden)


def adam_kernel(arrivals, core, own, *refs):
    others, refs = refs[:arrivals], refs[arrivals:]
    master, one, two = refs[:3]
    new_master, new_one, new_two, same, cross = refs[-5:]
    side, step = pl.program_id(0), pl.program_id(1)
    grad = own[...]
    for other in others:
        grad += other[0].astype(jnp.float32)
    first = beta_one * one[...] + (1.0 - beta_one) * grad
    second = beta_two * two[...] + (1.0 - beta_two) * grad * grad
    weights = master[...] - (learn_rate / fix_one) * first / (jnp.sqrt(second * (1.0 / fix_two)) + adam_eps)
    new_one[...] = first
    new_two[...] = second
    new_master[...] = weights
    height, width = weights.shape
    rows = same.shape[0] - SCALE_ROWS
    line = lax.broadcasted_iota(jnp.int32, (SCALE_ROWS, width), 0)

    def put(target):
        slab = target[rows:, :].astype(jnp.float32)
        for up in range(height // BLOCK):
            scales, values = [], []
            for across in range(width // BLOCK):
                block = weights[up * BLOCK : (up + 1) * BLOCK, across * BLOCK : (across + 1) * BLOCK]
                peak = jnp.max(jnp.max(jnp.abs(block), axis=0, keepdims=True), axis=1, keepdims=True)
                scale = (jnp.broadcast_to(peak, (1, BLOCK)) + scale_eps).astype(jnp.bfloat16).astype(jnp.float32)
                scales.append(scale)
                values.append((block * (1.0 / scale)).astype(jnp.bfloat16))
            at = step * height + up * BLOCK
            target[pl.ds(pl.multiple_of(at, BLOCK), BLOCK), :] = jnp.concatenate(values, axis=1)
            slab = jnp.where(line == at // BLOCK, jnp.concatenate(scales, axis=1), slab)
        target[rows:, :] = slab.astype(jnp.bfloat16)

    @pl.when(side == 0)
    def _():
        put(same)

    @pl.when(side == 1)
    def _():
        put(cross)


def adam(at, core, own, arrivals, master, one, two, before):
    j, chunks, width = at
    rows = own.shape[0]
    height = 2 * BLOCK if rows % (2 * BLOCK) == 0 else BLOCK
    side = lambda s, core: (core[0] + s) % 2
    state = pl.BlockSpec((height, width), lambda s, r, core: (r, side(s, core) * chunks + j))
    whole = jax.ShapeDtypeStruct(master.shape, jnp.float32)
    packed = jax.ShapeDtypeStruct((rows + SCALE_ROWS, width), jnp.bfloat16)
    packed_spec = pl.BlockSpec((rows + SCALE_ROWS, width), lambda s, r, core: (0, 0))
    count = len(arrivals)
    return pl.pallas_call(
        functools.partial(adam_kernel, count),
        grid_spec=pltpu.PrefetchScalarGridSpec(
            num_scalar_prefetch=1,
            grid=(2, rows // height),
            in_specs=[pl.BlockSpec((height, width), lambda s, r, core: (r, side(s, core)))]
            + [pl.BlockSpec((1, height, width), lambda s, r, core: (0, r, side(s, core)))] * count
            + [state] * 3
            + [pl.BlockSpec(memory_space=pl.ANY)] * len(before),
            out_specs=[state, state, state, packed_spec, packed_spec],
        ),
        out_shape=[whole, whole, whole, packed, packed],
        input_output_aliases={5 + count + i: i for i in range(len(before))},
        cost_estimate=pl.CostEstimate(
            flops=60 * rows * width, bytes_accessed=2 * rows * width * (30 + 2 * count), transcendentals=2 * rows * width
        ),
        name="adam",
    )(core, own, *arrivals, master, one, two, *before)


def place_kernel(count, table, core, *refs):
    pieces, (values, scales) = refs[:count], refs[-2:]
    rows = values.shape[0] // 2
    for k, piece in enumerate(pieces):

        @pl.when(pl.program_id(0) == k)
        def _():
            for i in range(2):
                spot = (core[0] + i) % 2
                values[pl.ds(pl.multiple_of(spot * rows, rows), rows), :] = piece[i, :rows, :]
                scales[spot] = piece[i, rows:, :]


def place(at, table, core, pieces, half, before):
    j, _, width = at
    count, (_, packed, _) = len(pieces), pieces[0].shape
    rows = packed - SCALE_ROWS
    return pl.pallas_call(
        functools.partial(place_kernel, count),
        grid_spec=pltpu.PrefetchScalarGridSpec(
            num_scalar_prefetch=2,
            grid=(count,),
            in_specs=[pl.BlockSpec((2, packed, width), lambda k, tab, core: (0, 0, 0))] * count
            + [pl.BlockSpec(memory_space=pl.ANY)] * len(before),
            out_specs=[
                pl.BlockSpec((2 * rows, width), lambda k, tab, core: (tab[k], j)),
                pl.BlockSpec((2, SCALE_ROWS, width), lambda k, tab, core: (tab[k], 0, j)),
            ],
        ),
        out_shape=[
            jax.ShapeDtypeStruct((2 * count * rows, half), jnp.bfloat16),
            jax.ShapeDtypeStruct((2 * count, SCALE_ROWS, half), jnp.bfloat16),
        ],
        input_output_aliases={2 + count + i: i for i in range(len(before))},
        cost_estimate=pl.CostEstimate(flops=0, bytes_accessed=8 * count * packed * width, transcendentals=0),
        name="place",
    )(table, core, *pieces, *before)


def cuts(blocks):
    sizes = [2] * (blocks // 2) + [1] * (blocks % 2)
    if blocks % 2 == 0:
        sizes[-1:] = [1, 1]
    chunks, start = [], 0
    for size in sizes:
        chunks.append((start // size, blocks // size, size * BLOCK))
        start += size
    return chunks


def plan(count, places):
    steps = []
    for i in range(min(2, count)):
        steps += [("product", i), ("hop", i, 0)]
    for i in range(count):
        steps.append(("hop", i, 1))
        if i >= 1:
            steps += [("adam", i - 1), ("plane", i - 1)]
        if i + 2 < count:
            steps += [("product", i + 2), ("hop", i + 2, 0)]
        steps += [("hop", i, k) for k in range(2, places - 1)]
        if i >= 2:
            steps.append(("gather", i - 2))
        if i >= 3:
            steps.append(("place", i - 3))
    steps += [("adam", count - 1), ("plane", count - 1)]
    for i in range(max(0, count - 2), count):
        steps.append(("gather", i))
        if i >= 1:
            steps.append(("place", i - 1))
    return steps + [("place", count - 1)]


def local(shards, groups, hidden, grad_out, master, moment_one, moment_two):
    places = shards // 2
    rows, half = master.shape[0], master.shape[1] // 2
    chunks = cuts(half // BLOCK)
    count = len(chunks)

    def permute(array, move):
        pairs = []
        for place, core, group in itertools.product(range(places), range(2), range(groups)):
            to = move(place, core, group)
            if to is not None:
                pairs.append(((place * 2 + core) * groups + group, (to[0] * 2 + to[1]) * groups + to[2]))
        return lax.ppermute(array, AXES, pairs)

    shard, group = lax.axis_index("fsdp"), lax.axis_index("tp")
    spot, core = shard // 2, shard % 2
    core_of = core.astype(jnp.int32).reshape(1)
    slots = jnp.arange(places)

    ahead = places - 1 - spot
    owner = jnp.where(slots < ahead, spot + 1 + slots, spot - 1 - (slots - ahead))
    owner = jnp.where(slots == places - 1, spot, owner).astype(jnp.int32)

    other_core = lambda p, c, t: (p, 1 - c, t)
    peer_hidden = permute(hidden, other_core)
    for_peer = turned((2 * slots + 1 - core).astype(jnp.int32), grad_out, rows)
    peer_grad = permute(for_peer, other_core)
    own_grad = turned((2 * slots + core).astype(jnp.int32), grad_out, rows)

    sends, own, arrivals, packed, pieces = {}, {}, {}, {}, {}
    state, shard_copy = [()], [()]

    def product(i):
        sends[i], own[i] = partial_products(chunks[i], owner, own_grad, peer_grad, hidden, peer_hidden)
        arrivals[i] = []

    def hop(i, k):
        payload = sends[i]
        if k:
            start = jnp.where(spot == k, 0, k)
            mine = lax.dynamic_slice_in_dim(payload, start, places - 1 - k, 0)
            payload = (mine.astype(jnp.float32) + arrivals[i][-1][1:].astype(jnp.float32)).astype(jnp.bfloat16)
        move = lambda p, c, t: (k + 1, c, t) if p == k else (places - 2 - k, c, t) if p == places - 1 - k else None
        arrivals[i].append(permute(payload, move))

    def update(i):
        *state[0], same, cross = adam(chunks[i], core_of, own[i], arrivals[i], master, moment_one, moment_two, state[0])
        packed[i] = (same, cross)

    def send(i):
        turn = i % groups
        same, cross = packed[i]
        packed[i] = (
            permute(same, lambda p, c, t: (t, c, p ^ turn)), permute(cross, lambda p, c, t: (t, 1 - c, p ^ turn))
        )

    def gather(i):
        both = jnp.stack(packed[i])
        pieces[i] = [both] + [permute(both, lambda p, c, t: (p, c, t ^ m)) for m in range(1, groups)]

    def put(i):
        sources = (group ^ slots ^ (i % groups)).astype(jnp.int32)
        shard_copy[0] = place(chunks[i], sources, core_of, pieces[i], half, shard_copy[0])

    actions = {"product": product, "hop": hop, "adam": update, "plane": send, "gather": gather, "place": put}
    for name, *where in plan(count, places):
        actions[name](*where)

    quantized, scales = shard_copy[0]
    lines, blocks = rows // BLOCK, half // BLOCK
    block_scales = scales[:, :lines].reshape(shards * lines, blocks, BLOCK)[:, :, 0]
    return (*state[0], quantized, block_scales)


def solution(mesh):
    shards, groups = mesh.shape["fsdp"], mesh.shape["tp"]
    assert shards == 2 * groups and groups & (groups - 1) == 0

    def body(*args):
        return local(shards, groups, *args)

    return jax.shard_map(
        body,
        mesh=mesh,
        in_specs=(
            P("fsdp", "tp"),
            P("fsdp", None),
            P("fsdp", "tp"),
            P("fsdp", "tp"),
            P("fsdp", "tp"),
        ),
        out_specs=(
            P("fsdp", "tp"),
            P("fsdp", "tp"),
            P("fsdp", "tp"),
            P(None, "fsdp"),
            P(None, "fsdp"),
        ),
        check_vma=False,
    )
```
